128 devices in a mesh: elem: 8 (over y, core), bin: 16 (over z, x).
Axes of the slice: x: 4, y: 4, z: 4, core: 2. Of those that a mesh axis runs over, the one named last changes fastest.
Arguments:
- source: float32 [3, 128, 256, 128], P(None, 'elem', 'bin'), may hold values from -60 to 60
- viscosity: float32 [128, 256, 128], P('elem', 'bin'), may hold values from 0.3 to 3
- coarse_inverse: float32 [8, 128, 128], P('elem', 'bin'), may hold values from -0.06187184 to 2, as said below
- droplets: float32 [7, 8, 65536], P(None, 'elem', 'bin'), may hold values from -3 to 3, as said below
- droplet_elem: int32 [8, 65536], P('elem', 'bin'), may hold values from 0 to 63
- ghost_counts: int32 [2, 8, 16], P(None, 'elem', 'bin'), may hold values from 1 to 8, as said below
- tile_pairs: int32 [2, 8, 4096], P(None, 'elem', 'bin'), may hold values from 0 to 47, as said below
- tile_count: int32 [8, 16], P('elem', 'bin'), may hold values from 32 to 256, as said below
Outputs:
- velocity: float32 [3, 128, 256, 128], P(None, 'elem', 'bin')
- droplet_velocity: float32 [3, 8, 65536], P(None, 'elem', 'bin')
The draws below stay inside these ranges and needn't reach their ends.
Inputs may be any that keep to these rules, and one draw needn't show every extreme that they name: `ghost_counts`: at least one bin sends 8 blocks to its lower neighbour and one to its upper neighbour. `tile_pairs`: row 0 names own blocks, below 32; row 1 names candidate blocks. `tile_count`: some bin uses all 256 tile slots. `droplets`: positions x, z and y lie in 0 to 1, diameters in 0.5 to 1.5. `coarse_inverse`: diagonal entries lie in 1 to 2.
All inputs are finite; a program needn't handle non-finite values.
Results may differ from the reference program's by a relative error of at most 0.0003.
Values sent between devices are 32-bit elements; how exact they have to be, the bound alone decides.
A program may use at most 128 MiB of HBM per device.

```python
import math
import jax
import jax.numpy as jnp
import numpy as np
from jax import lax

EX = 2
EY = 2
EZ = 16
ITERS = 4
NB = 32
BLOCK = 128
GMAX = 8
TGROUP = 16
TMAX = 256
ROWS = 4096
LINES = 8
BINS = 16
DROPS = 65536
NXN = 128
NYN = 256
NZN = 128
GC = 128


def draw_droplets(key, part):
    subkeys = jax.random.split(key, 4)
    local = (jnp.arange(DROPS, dtype=jnp.int32) % ROWS).astype(jnp.float32)
    jitter = jax.random.uniform(subkeys[0], (LINES, DROPS), jnp.float32)
    height = (local[None, :] + jitter) / ROWS
    across = jax.random.uniform(subkeys[1], (2, LINES, DROPS), jnp.float32)
    speeds = jnp.clip(jax.random.normal(subkeys[2], (3, LINES, DROPS), jnp.float32), -3.0, 3.0)
    diameter = jax.random.uniform(subkeys[3], (LINES, DROPS), jnp.float32, 0.5, 1.5)
    return jnp.stack([across[0], height, across[1], speeds[0], speeds[1], speeds[2], diameter], 0)


def draw_ghost_counts(key, part):
    subkeys = jax.random.split(key, 3)
    counts = jax.random.randint(subkeys[0], (2, LINES, BINS), 1, GMAX + 1)
    line_pick = jax.random.randint(subkeys[1], (2,), 0, LINES)
    bin_pick = jax.random.randint(subkeys[2], (2,), 0, BINS)
    counts = counts.at[0, line_pick[0], bin_pick[0]].set(GMAX)
    counts = counts.at[1, line_pick[1], bin_pick[1]].set(GMAX)
    return counts.astype(jnp.int32)


def draw_tile_pairs(key, part):
    subkeys = jax.random.split(key, 2)
    own_block = jax.random.randint(subkeys[0], (LINES, BINS * TMAX), 0, NB)
    offset = jax.random.randint(subkeys[1], (LINES, BINS * TMAX), -GMAX, GMAX + 1)
    reach = own_block + offset
    cand_block = jnp.where(reach < 0, NB + GMAX + reach, jnp.where(reach >= NB, reach + GMAX, reach))
    return jnp.stack([own_block, cand_block], 0).astype(jnp.int32)


def draw_tile_count(key, part):
    subkeys = jax.random.split(key, 3)
    counts = jax.random.randint(subkeys[0], (LINES, BINS), TMAX // 8, TMAX // 2 + 1)
    line_pick = jax.random.randint(subkeys[1], (), 0, LINES)
    bin_pick = jax.random.randint(subkeys[2], (), 0, BINS)
    return counts.at[line_pick, bin_pick].set(TMAX).astype(jnp.int32)


def draw_coarse_inverse(key, part):
    subkeys = jax.random.split(key, 2)
    row_ids = jnp.arange(GC, dtype=jnp.int32)[:, None]
    col_ids = jnp.arange(GC, dtype=jnp.int32)[None, :]
    outside = jax.random.uniform(subkeys[0], (LINES, GC, GC), jnp.float32, -1.0, 1.0) * (0.7 / math.sqrt(GC))
    diagonal = jax.random.uniform(subkeys[1], (LINES, GC, GC), jnp.float32, 1.0, 2.0)
    return jnp.where((row_ids == col_ids)[None, :, :], diagonal, outside)


def with_ends(values, key, low, top_value):
    dims = values.shape
    index_at = [jax.random.randint(jax.random.fold_in(key, axis), (), 0, dims[axis]) for axis in range(len(dims))]
    values = values.at[tuple(index_at)].set(low)
    longest = dims.index(max(dims))
    index_at[longest] = (index_at[longest] + 1) % dims[longest]
    return values.at[tuple(index_at)].set(top_value)


def block_scale(key, dims, cuts, low, largest):
    def one(dim, parts):
        steps = jax.random.uniform(jax.random.fold_in(jax.random.fold_in(key, 6), dim), (parts,), jnp.float32, low / len(cuts), largest / len(cuts))
        return jnp.repeat(jnp.exp(steps), dims[dim] // parts).reshape((-1,) + (1,) * (len(dims) - dim - 1))

    level = one(*cuts[0])
    for cut in cuts[1:]:
        level = level * one(*cut)
    return level


def normal_values(stream_key, dims, scale, most, cuts=(), kind=jnp.bfloat16):
    factor_of = block_scale(stream_key, dims, cuts, -0.22, 0.18) if cuts else 1.0
    drawn = jax.random.normal(stream_key, dims, jnp.float32) * scale * factor_of
    return jnp.minimum(jnp.maximum(drawn, -most), most).astype(kind)


def setup_inputs(seed: int = 0) -> dict:
    key_list = jax.random.split(jax.random.key(seed), 9)
    return {
        "source": normal_values(key_list[0], (3, NXN, NYN, NZN), 10.0, 60.0, ((1, 8), (2, 16)), jnp.float32),
        "viscosity": jnp.clip(jnp.exp(math.log(3.0) - 2.3025851 * jax.random.uniform(key_list[1], (NXN, NYN, NZN), jnp.float32) ** block_scale(key_list[1], (NXN, NYN, NZN), ((0, 8), (1, 16)), -0.2, 0.2)), 0.3, 3.0),
        "coarse_inverse": draw_coarse_inverse(jax.random.fold_in(key_list[8], 71), 0),
        "droplets": draw_droplets(jax.random.fold_in(key_list[8], 71), 0),
        "droplet_elem": with_ends(jax.random.randint(key_list[4], (LINES, DROPS), 0, EX * EY * EZ), jax.random.fold_in(key_list[4], 1), 0, (EX * EY * EZ) - 1).astype(jnp.int32),
        "ghost_counts": draw_ghost_counts(jax.random.fold_in(key_list[8], 71), 0),
        "tile_pairs": draw_tile_pairs(jax.random.fold_in(key_list[8], 71), 0),
        "tile_count": draw_tile_count(jax.random.fold_in(key_list[8], 71), 0),
    }


PRECISE = lax.Precision.HIGHEST
MASS_TERM = 1.0
RELAXATION = 0.6
COARSE_GAIN = 0.02
SPREAD = 0.1
STIFFNESS = 0.3
TIME_STEP = 0.1


def legendre_top(points):
    previous = points * 0.0 + 1.0
    current = points * 1.0
    for degree_index in range(1, 7):
        following = ((2 * degree_index + 1) * points * current - degree_index * previous) / (degree_index + 1)
        previous = current
        current = following
    return current


def gll_tables():
    points = np.array([-1.0, -0.8717401485096066, -0.5917001814331423, -0.2092992179024789, 0.2092992179024789, 0.5917001814331423, 0.8717401485096066, 1.0])
    weights = np.array([0.03571428571428571, 0.2107042271435061, 0.3411226924835044, 0.4124587946587038, 0.4124587946587038, 0.3411226924835044, 0.2107042271435061, 0.03571428571428571])
    legendre = legendre_top(points)
    derivative = np.zeros((8, 8))
    for row_index in range(8):
        for col_index in range(8):
            if row_index != col_index:
                derivative[row_index, col_index] = legendre[row_index] / legendre[col_index] / (points[row_index] - points[col_index])
    derivative[0, 0] = -14.0
    derivative[7, 7] = 14.0
    return derivative.astype(np.float32), weights.astype(np.float32)


def seam_counts():
    return np.array([2.0, 1.0, 1.0, 1.0, 1.0, 1.0, 1.0, 2.0], np.float32)


def node_line(values, length):
    return jnp.asarray(np.tile(values, length // 8))


def nodal(line_x, line_y, line_z):
    return line_x[:, None, None] * line_y[None, :, None] * line_z[None, None, :]


def along(values, direction, matrix):
    amount = values.shape[direction] // 8
    divided = values.reshape(values.shape[:direction] + (amount, 8) + values.shape[direction + 1:])
    contracted = jnp.tensordot(divided, matrix, axes=((direction + 1,), (1,)), precision=PRECISE)
    return jnp.moveaxis(contracted, -1, direction + 1).reshape(values.shape)


def seam_pass(values, direction, lower_plane, upper_plane):
    amount = values.shape[direction] // 8
    divided = values.reshape(values.shape[:direction] + (amount, 8) + values.shape[direction + 1:])
    first_nodes = lax.index_in_dim(divided, 0, direction + 1, keepdims=False)
    last_nodes = lax.index_in_dim(divided, 7, direction + 1, keepdims=False)
    upper_sum = last_nodes + jnp.concatenate([lax.slice_in_dim(first_nodes, 1, amount, axis=direction), upper_plane], direction)
    lower_sum = jnp.concatenate([lower_plane, lax.slice_in_dim(last_nodes, 0, amount - 1, axis=direction)], direction) + first_nodes
    inner = lax.slice_in_dim(divided, 1, 7, axis=direction + 1)
    joined = jnp.concatenate([jnp.expand_dims(lower_sum, direction + 1), inner, jnp.expand_dims(upper_sum, direction + 1)], direction + 1)
    return joined.reshape(values.shape)


def assemble_whole(values):
    for direction in (1, 2, 3):
        length = values.shape[direction]
        values = seam_pass(values, direction, lax.slice_in_dim(values, length - 1, length, axis=direction), lax.slice_in_dim(values, 0, 1, axis=direction))
    return values


def prolong(coarse_cells):
    extent = coarse_cells.shape
    spread_cells = jnp.broadcast_to(coarse_cells[:, :, None, :, None, :, None], (extent[0], extent[1], 16, extent[2], 16, extent[3], 16))
    return spread_cells.reshape(extent[0], extent[1] * 16, extent[2] * 16, extent[3] * 16)


def tile_force(candidates, own_block, cand_block, active):
    near_rows = candidates[own_block]
    far_rows = candidates[cand_block]
    distance = jnp.zeros((near_rows.shape[0], near_rows.shape[2], far_rows.shape[2]), jnp.float32)
    for component in range(3):
        offset = near_rows[:, component, :, None] - far_rows[:, component, None, :]
        distance = distance + offset * offset
    kernel = jnp.exp(-distance / SPREAD) * far_rows[:, 3, None, :] * active[:, None, None]
    summed = jnp.sum(kernel, axis=2)
    pulled = jnp.einsum("tab,tcb->tca", kernel, far_rows[:, :3], precision=PRECISE)
    return STIFFNESS * near_rows[:, 3, None, :] * (near_rows[:, :3] * summed[:, None, :] - pulled)


def collide_padded(candidates, tile_ids, limit):
    groups = tile_ids.shape[1] // TGROUP
    own_blocks = tile_ids[0].reshape(groups, TGROUP)
    cand_blocks = tile_ids[1].reshape(groups, TGROUP)
    positions = jnp.arange(groups * TGROUP, dtype=jnp.int32).reshape(groups, TGROUP)

    def advance(collision, entries):
        own_block, cand_block, position = entries
        active = (position < limit).astype(jnp.float32)
        return collision.at[own_block].add(tile_force(candidates, own_block, cand_block, active)), None

    start_value = jnp.zeros((NB, 3, candidates.shape[2]), jnp.float32)
    collision, unused = lax.scan(advance, start_value, (own_blocks, cand_blocks, positions))
    return collision


def mask_size(part, kept):
    return jnp.concatenate([part[:3], part[3:] * kept[None, :]], 0)


def shift_height(part, amount):
    return jnp.concatenate([part[:1], part[1:2] + amount, part[2:]], 0)


def drop_position(drops):
    return jnp.stack([drops[0], drops[1], drops[2], drops[6]])


def per_device(device_items):
    own_drops, below_drops, above_drops, below_upper, above_lower, elem_ids, tile_ids, limit, element_mean = device_items
    span = GMAX * BLOCK
    block_ids = jnp.arange(span, dtype=jnp.int32) // BLOCK
    position = drop_position(own_drops)
    from_below = shift_height(mask_size(drop_position(below_drops)[:, -span:], (block_ids >= GMAX - below_upper).astype(jnp.float32)), -1.0)
    from_above = shift_height(mask_size(drop_position(above_drops)[:, :span], (block_ids < above_lower).astype(jnp.float32)), 1.0)
    candidates = jnp.concatenate([position, from_below, from_above], 1).reshape(4, NB + 2 * GMAX, BLOCK).transpose(1, 0, 2)
    collision = collide_padded(candidates, tile_ids, limit).transpose(1, 0, 2).reshape(3, ROWS)
    sampled = jnp.take(element_mean, elem_ids, axis=1)
    speeds = own_drops[3:6]
    diameter = own_drops[6]
    return speeds + TIME_STEP * ((sampled - speeds) / (diameter * diameter) + collision)


def flatten_devices(values):
    return values.reshape((LINES * BINS,) + values.shape[2:])


def reference(source, viscosity, coarse_inverse, droplets, droplet_elem, ghost_counts, tile_pairs, tile_count):
    derivative, weights = gll_tables()
    deriv_table = jnp.asarray(derivative)
    square_table = deriv_table * deriv_table
    components, width_x, width_y, width_z = source.shape
    weight = nodal(node_line(weights, width_x), node_line(weights, width_y), node_line(weights, width_z))
    multiplicity = nodal(node_line(seam_counts(), width_x), node_line(seam_counts(), width_y), node_line(seam_counts(), width_z))
    coef_w = viscosity * weight

    def apply_local(component_field):
        summed = MASS_TERM * weight * component_field
        for direction in range(3):
            gradient = along(component_field, direction, deriv_table)
            summed = summed + along(coef_w * gradient, direction, deriv_table.T)
        return summed

    diagonal_local = MASS_TERM * weight
    for direction in range(3):
        diagonal_local = diagonal_local + along(coef_w, direction, square_table.T)
    diag_sum = assemble_whole(diagonal_local[None])[0]
    forcing = weight * source
    velocity = jnp.zeros_like(source)
    for sweep_index in range(ITERS):
        if sweep_index == 0:
            residual = assemble_whole(forcing)
        else:
            residual = assemble_whole(forcing - lax.map(apply_local, velocity))
        coarse = (weight * residual / multiplicity).reshape(components, width_x // 16, 16, width_y // 16, 16, width_z // 16, 16).sum(axis=(2, 4, 6))
        coarse = coarse.reshape(components, LINES, EX // 2, BINS, EY // 2, EZ // 2).transpose(0, 1, 3, 2, 4, 5).reshape(components, LINES, GC)
        coarse_dual = jnp.einsum("egh,ceg->ceh", coarse_inverse, coarse, precision=PRECISE)
        correction = jnp.einsum("egh,ceh->ceg", coarse_inverse, coarse_dual, precision=PRECISE)
        correction = correction.reshape(components, LINES, BINS, EX // 2, EY // 2, EZ // 2).transpose(0, 1, 3, 2, 4, 5)
        correction = correction.reshape(components, width_x // 16, width_y // 16, width_z // 16)
        velocity = velocity + assemble_whole((RELAXATION * residual / diag_sum + COARSE_GAIN * prolong(correction)) / multiplicity)
    element_mean = (weight * velocity).reshape(components, width_x // 8, 8, width_y // 8, 8, width_z // 8, 8).sum(axis=(2, 4, 6)) / 8.0
    means = element_mean.reshape(components, LINES, EX, BINS, EY, EZ).transpose(1, 3, 0, 2, 4, 5).reshape(LINES, BINS, components, EX * EY * EZ)
    drops = droplets.reshape(7, LINES, BINS, ROWS).transpose(1, 2, 0, 3)
    below_drops = jnp.roll(drops, 1, axis=1)
    above_drops = jnp.roll(drops, -1, axis=1)
    below_upper = jnp.roll(ghost_counts[1], 1, axis=1)
    above_lower = jnp.roll(ghost_counts[0], -1, axis=1)
    elem_ids = droplet_elem.reshape(LINES, BINS, ROWS)
    tile_ids = tile_pairs.reshape(2, LINES, BINS, TMAX).transpose(1, 2, 0, 3)
    device_items = (flatten_devices(drops), flatten_devices(below_drops), flatten_devices(above_drops), flatten_devices(below_upper), flatten_devices(above_lower), flatten_devices(elem_ids), flatten_devices(tile_ids), flatten_devices(tile_count), flatten_devices(means))
    updated = lax.map(per_device, device_items)
    droplet_velocity = updated.reshape(LINES, BINS, 3, ROWS).transpose(2, 0, 1, 3).reshape(3, LINES, DROPS)
    return (velocity, droplet_velocity)
```

```python
import functools

import jax
import jax.numpy as jnp
import numpy as np
from jax import lax
from jax.experimental import pallas as pl
from jax.experimental.pallas import tpu as pltpu
from jax.sharding import PartitionSpec as P

ITERS = 4
NB = 32
GMAX = 8
NCAND = NB + 2 * GMAX
TMAX = 256
KF = 32
MESH = pl.DeviceIdType.MESH

RELAXATION = 0.6
COARSE_GAIN = 0.02
STIFFNESS = 0.3
TIME_STEP = 0.1
ALPHA = float(np.log2(np.e) / 0.1)

F32 = jnp.float32
BF16 = jnp.bfloat16


def legendre_top(points):
    previous = points * 0.0 + 1.0
    current = points * 1.0
    for degree in range(1, 7):
        following = ((2 * degree + 1) * points * current - degree * previous) / (degree + 1)
        previous = current
        current = following
    return current


def gll_tables():
    half = [-1.0, -0.8717401485096066, -0.5917001814331423, -0.2092992179024789]
    points = np.array(half + [-value for value in reversed(half)])
    half = [0.03571428571428571, 0.2107042271435061, 0.3411226924835044, 0.4124587946587038]
    weights = np.array(half + list(reversed(half)))
    legendre = legendre_top(points)
    derivative = np.zeros((8, 8))
    for row in range(8):
        for col in range(8):
            if row != col:
                derivative[row, col] = (
                    legendre[row] / legendre[col] / (points[row] - points[col])
                )
    derivative[0, 0] = -14.0
    derivative[7, 7] = 14.0
    return derivative.astype(np.float32), weights.astype(np.float32)


DERIV, WEIGHTS = gll_tables()
COUNTS = np.array([2.0, 1.0, 1.0, 1.0, 1.0, 1.0, 1.0, 2.0], np.float32)
SHARE = WEIGHTS / COUNTS


def roll_tables(matrix):
    out = np.zeros((8, 8, 128), np.float32)
    for k in range(8):
        for i in range(8):
            out[k, i, :] = matrix[i, (i - k) % 8]
    return out


def vector_tables():
    wz = np.tile(WEIGHTS, 16)
    sz = np.tile(SHARE, 16)
    planes = [(WEIGHTS[:, None] * wz[None, :])[None], (SHARE[:, None] * sz[None, :])[None]]
    square = DERIV * DERIV
    planes += [roll_tables(DERIV), roll_tables(DERIV.T), roll_tables(square.T)]
    return np.concatenate(planes, 0).astype(np.float32)


def lane_tables():
    out = []
    identity = np.eye(16, dtype=np.float32)
    for matrix in (DERIV.T, DERIV, DERIV * DERIV):
        full = np.kron(identity, matrix)
        high = full.astype(jnp.bfloat16)
        low = (full - high.astype(np.float32)).astype(jnp.bfloat16)
        zero = np.zeros_like(low)
        top = np.concatenate([high, low], 1)
        out.append(np.concatenate([top, np.concatenate([high, zero], 1)], 0))
    return np.stack(out)


def split2(x):
    high = x.astype(BF16)
    return high, (x - high.astype(F32)).astype(BF16)


def split3(x):
    high = x.astype(BF16)
    rest = x - high.astype(F32)
    middle = rest.astype(BF16)
    return high, middle, (rest - middle.astype(F32)).astype(BF16)


def split3_wide(x):
    return [part.astype(F32) for part in split3(x)]


def mm(a, b):
    return jnp.dot(a, b, preferred_element_type=F32)


def lane_product(x, table):
    high, low = split2(x)
    both = mm(jnp.concatenate([high, low], 1), table)
    return both[:, :128] + both[:, 128:]


def exact_product(x, ones):
    rows = x.shape[0]
    out = mm(jnp.concatenate(split3(x), 0), ones)
    return out[:rows] + out[rows : 2 * rows] + out[2 * rows : 3 * rows]


def iota(shape, dim):
    return lax.broadcasted_iota(jnp.int32, shape, dim)


def kernel(
    n_elem,
    n_bin,
    tp_s,
    cnt_s,
    gc_s,
    src,
    visc,
    xin,
    drops,
    elem,
    own_v,
    tab,
    ztab,
    vel,
    dvel,
    coef,
    dinv,
    q,
    r,
    ysend,
    esend,
    xrecv,
    yrecv,
    erecv,
    rcs,
    crecv,
    xsend,
    xgat,
    wmat,
    gsend,
    grecv,
    nearf,
    farf,
    pf,
    near,
    far,
    pb,
    raw,
    oh,
    samp,
    hsend,
    hrecv,
    csend,
    crsem,
    xssem,
    xrsem,
    gssem,
    grsem,
):
    e = lax.axis_index("elem")
    b = lax.axis_index("bin")
    em, ep = lax.rem(e + n_elem - 1, n_elem), lax.rem(e + 1, n_elem)
    bm, bp = lax.rem(b + n_bin - 1, n_bin), lax.rem(b + 1, n_bin)
    total = 3 * n_bin - 1

    def each_partner(act):
        for de, row in ((0, e), (1, ep), (-1, em)):

            def step(db, carry, row=row, de=de):
                act(de, row, lax.rem(b + db, n_bin))
                return carry

            lax.fori_loop(1 if de == 0 else 0, n_bin, step, 0)

    barrier = pltpu.get_barrier_semaphore()
    each_partner(
        lambda de, row, col: pl.semaphore_signal(
            barrier, inc=1, device_id=(row, col), device_id_type=MESH
        )
    )

    lane = iota((8, 128), 1)
    sub = iota((8, 128), 0)
    lane8 = lax.rem(lane, 8)
    first_lane, last_lane = lane8 == 0, lane8 == 7
    first_sub, last_sub = sub == 0, sub == 7
    wyz = tab[0]
    syz = tab[1]

    def seam_z(v):
        up = pltpu.roll(v, 127, 1)
        down = pltpu.roll(v, 1, 1)
        return v + jnp.where(last_lane, up, jnp.where(first_lane, down, 0.0))

    def seam_inner(c, planes):
        out = []
        for low, high in planes:
            low, high = seam_z(low), seam_z(high)
            new_low = low + jnp.where(last_sub, pltpu.roll(high, 7, 0), 0.0)
            new_high = high + jnp.where(first_sub, pltpu.roll(low, 1, 0), 0.0)
            out.append((new_low, new_high))
        return out

    def store_planes(c, get):
        held = None
        for x in range(16):
            low, high = seam_inner(c, [get(x)])[0]
            if x == 7:
                held = (low, high)
                continue
            if x == 8:
                low, high = held[0] + low, held[1] + high
                q[c, 7, 0:8, :] = low
                q[c, 7, 8:16, :] = high
            q[c, x, 0:8, :] = low
            q[c, x, 8:16, :] = high

    def contract_rows(v, base):
        out = tab[base] * v
        for k in range(1, 8):
            out = out + tab[base + k] * pltpu.roll(v, k, 0)
        return out

    for x in range(16):
        for half in range(2):
            rows = pl.ds(8 * half, 8)
            coef[x, rows, :] = visc[x, rows, :] * (wyz * float(WEIGHTS[x % 8]))

    diag_z = lane_product(coef[...].reshape(256, 128), ztab[2])
    r[3] = diag_z.reshape(16, 16, 128)

    def diag_at(x):
        out = []
        for half in range(2):
            rows = pl.ds(8 * half, 8)
            total_d = r[3, x, rows, :] + wyz * float(WEIGHTS[x % 8])
            total_d = total_d + contract_rows(coef[x, rows, :], 18)
            start = (x // 8) * 8
            for i in range(8):
                factor = float(DERIV[i, x % 8] * DERIV[i, x % 8])
                total_d = total_d + factor * coef[start + i, rows, :]
            out.append(total_d)
        return tuple(out)

    store_planes(3, diag_at)

    def force_comp(c, carry):
        store_planes(
            c,
            lambda x: tuple(
                src[c, x, pl.ds(8 * half, 8), :] * (wyz * float(WEIGHTS[x % 8]))
                for half in range(2)
            ),
        )
        return carry

    lax.fori_loop(0, 3, force_comp, 0)

    q2 = q.reshape(4 * 256, 128)
    r2 = r.reshape(4 * 256, 128)
    edges = ((0, 0), (0, 15), (15, 0), (15, 15))

    def halo_copies(k, comps):
        side = pl.ds(0, comps)
        flat = pl.ds(0, comps * 16)

        def remote(src_ref, dst_ref, index, row, col):
            return pltpu.make_async_remote_copy(
                src_ref=src_ref,
                dst_ref=dst_ref,
                send_sem=hsend.at[k, index],
                recv_sem=hrecv.at[k, index],
                device_id=(row, col),
                device_id_type=MESH,
            )

        copies = [
            remote(q.at[side, 0], xrecv.at[k, 1, side], 0, em, b),
            remote(q.at[side, 15], xrecv.at[k, 0, side], 1, ep, b),
            remote(ysend.at[k, 0, flat], yrecv.at[k, 1, flat], 2, e, bm),
            remote(ysend.at[k, 1, flat], yrecv.at[k, 0, flat], 3, e, bp),
        ]
        for index, (x, y) in enumerate(edges):
            row = em if x == 0 else ep
            col = bm if y == 0 else bp
            copies.append(
                remote(esend.at[k, index], erecv.at[k, 3 - index], 4 + index, row, col)
            )
        return copies

    def halo_start(k, comps):
        ysend[k, 0, 0 : comps * 16, :] = q2[pl.ds(0, comps * 16, stride=16), :]
        ysend[k, 1, 0 : comps * 16, :] = q2[pl.ds(15, comps * 16, stride=16), :]
        for index, (x, y) in enumerate(edges):
            for c in range(4):
                if c < comps:
                    esend[k, index, c : c + 1, :] = q[c, x, y : y + 1, :]
                else:
                    esend[k, index, c : c + 1, :] = jnp.zeros((1, 128), F32)
        copies = halo_copies(k, comps)
        for copy in copies:
            copy.start()
        return copies

    def halo_finish(k, comps, copies):
        for copy in copies:
            copy.wait_recv()
        for c in range(comps):
            r[c, 1:15] = q[c, 1:15]
            r[c, 0] = q[c, 0] + xrecv[k, 0, c]
            r[c, 15] = q[c, 15] + xrecv[k, 1, c]
        low = pl.ds(0, comps * 16, stride=16)
        high = pl.ds(15, comps * 16, stride=16)
        r2[low, :] = r2[low, :] + yrecv[k, 0, 0 : comps * 16, :]
        r2[high, :] = r2[high, :] + yrecv[k, 1, 0 : comps * 16, :]
        for index, (x, y) in enumerate(edges):
            for c in range(comps):
                r[c, x, y : y + 1, :] = r[c, x, y : y + 1, :] + erecv[k, index, c : c + 1, :]

    fields = (0, 1, 2, 6)
    keep_low = (sub < gc_s[0]).astype(F32)
    keep_high = (sub >= GMAX - gc_s[1]).astype(F32)
    for index, field in enumerate(fields):
        low = drops[field, 0:GMAX, :]
        high = drops[field, NB - GMAX : NB, :]
        if field == 6:
            low, high = low * keep_low, high * keep_high
        gsend[0, index] = low
        gsend[1, index] = high
    xsend[...] = xin[0]

    pl.semaphore_wait(barrier, total)

    halos = [None] * ITERS
    halos[0] = halo_start(0, 4)
    ghosts = []
    for side, col in ((0, bm), (1, bp)):
        copy = pltpu.make_async_remote_copy(
            src_ref=gsend.at[side],
            dst_ref=grecv.at[1 - side],
            send_sem=gssem.at[side],
            recv_sem=grsem.at[side],
            device_id=(e, col),
            device_id_type=MESH,
        )
        copy.start()
        ghosts.append(copy)

    def send_x(de, row, col):
        pltpu.make_async_remote_copy(
            src_ref=xsend,
            dst_ref=xgat.at[(1 - de) * n_bin + b],
            send_sem=xssem.at[0],
            recv_sem=xrsem.at[0],
            device_id=(row, col),
            device_id_type=MESH,
        ).start()

    each_partner(send_x)

    def features(shape_rows, x, y, z, s):
        pass

    def near_rows(start, x, y, z):
        count = x.shape[0]
        place = lambda k: pl.ds(start * KF + k, count, stride=KF)
        k = 0
        for value in (x, y, z):
            high, middle, low = split3_wide(value * (2.0 * ALPHA))
            for part in (high, high, high, middle, middle, low):
                nearf[place(k), :] = part
                k += 1
        for part in split3_wide((x * x + y * y + z * z) * (-ALPHA)):
            nearf[place(k), :] = part
            k += 1
        for k in range(k, KF):
            value = 1.0 if k < 24 else 0.0
            nearf[place(k), :] = jnp.full(x.shape, value, F32)

    def far_rows(start, x, y, z, s):
        count = x.shape[0]
        place = lambda k: pl.ds(start * KF + k, count, stride=KF)
        k = 0
        for value in (x, y, z):
            high, middle, low = split3_wide(value)
            for part in (high, middle, low, high, middle, high):
                farf[place(k), :] = part
                k += 1
        for k in range(k, k + 3):
            farf[place(k), :] = jnp.full(x.shape, 1.0, F32)
        k += 1
        for part in split3_wide((x * x + y * y + z * z) * (-ALPHA)):
            farf[place(k), :] = part
            k += 1
        for k in range(k, KF):
            farf[place(k), :] = jnp.full(x.shape, 0.0, F32)
        for index, value in enumerate((s, s * x, s * y, s * z)):
            for level, part in enumerate(split3_wide(value)):
                pf[pl.ds(start * 16 + level * 4 + index, count, stride=16), :] = part
        for index in range(12, 16):
            pf[pl.ds(start * 16 + index, count, stride=16), :] = jnp.full(x.shape, 0.0, F32)

    def far_finish(start, groups):
        def step(g, carry):
            rows = pl.multiple_of((start + g * 4) * KF, 128)
            turned = farf[pl.ds(rows, 128), :].T
            for u in range(4):
                far[start + g * 4 + u] = turned[:, u * KF : (u + 1) * KF].astype(BF16)
            rows = pl.multiple_of((start + g * 4) * 16, 64)
            part = pf[pl.ds(rows, 64), :].astype(BF16).reshape(4, 16, 128)
            pb[pl.ds(start + g * 4, 4), :, 0:128] = part
            pb[pl.ds(start + g * 4, 4), :, 128:256] = part
            return carry

        lax.fori_loop(0, groups, step, 0)

    xa, ya, za, sa = drops[0] - 0.5, drops[1] - 0.5, drops[2] - 0.5, drops[6]
    near_rows(0, xa, ya, za)
    near[...] = nearf[...].astype(BF16).reshape(NB, KF, 128)
    far_rows(0, xa, ya, za, sa)
    far_finish(0, NB // 4)

    def onehot(i, carry):
        row = jnp.broadcast_to(elem[pl.ds(i, 1), :], (64, 128))
        oh[i] = (row == iota((64, 128), 0)).astype(F32).astype(BF16)
        return carry

    lax.fori_loop(0, NB, onehot, 0)

    for copy in ghosts:
        copy.wait_recv()
    far_rows(NB, grecv[0, 0] - 0.5, grecv[0, 1] - 1.5, grecv[0, 2] - 0.5, grecv[0, 3])
    far_rows(
        NB + GMAX, grecv[1, 0] - 0.5, grecv[1, 1] + 0.5, grecv[1, 2] - 0.5, grecv[1, 3]
    )
    far_finish(NB, 2 * GMAX // 4)

    def tiles(first, count, unroll=8):
        def step(i, carry):
            for j in range(unroll):
                t = first + i * unroll + j
                own, cand = tp_s[0, t], tp_s[1, t]
                g = jnp.exp2(mm(far[cand], near[own]))
                high, low = split2(g)
                out = mm(pb[cand], jnp.concatenate([high, low], 0))
                raw[pl.ds(pl.multiple_of(t * 16, 16), 16), :] = out
            return carry

        lax.fori_loop(0, count // unroll, step, 0)

    def coarse_setup():
        pltpu.make_async_copy(
            xgat.at[pl.ds(0, total)], xgat.at[pl.ds(0, total)], xrsem.at[0]
        ).wait()
        xgat[n_bin + b] = xsend[...]
        g, z = iota((128, 128), 0), iota((128, 128), 1)
        bin_of, cell = g // 8, lax.rem(g, 8)
        z_cell, z_in = z // 16, lax.rem(z, 16)
        other = jnp.where(z_in == 0, lax.rem(z_cell + 7, 8), lax.rem(z_cell + 1, 8))
        at_face = jnp.logical_or(z_in == 0, z_in == 15)
        value = jnp.where(cell == z_cell, jnp.where(at_face, 0.5, 1.0), 0.0)
        value = value + jnp.where(jnp.logical_and(at_face, cell == other), 0.5, 0.0)
        pick = lambda which: jnp.where(bin_of == which, value, 0.0)
        here = pick(b)
        spread = jnp.concatenate(
            [0.5 * (here + pick(bm)), here, 0.5 * (here + pick(bp))], 1
        ).astype(BF16)

        def line(l, carry):
            x = xgat[pl.ds(l * n_bin, n_bin)].reshape(128, 128)
            high, low = split2(x)
            turn = lambda p, w: lax.dot_general(
                p, w, (((1,), (1,)), ((), ())), preferred_element_type=F32
            )
            gram = turn(high, high) + turn(high, low) + turn(low, high)
            a, c2 = split2(exact_product(gram, spread))
            wmat[l, :, 0:384] = a
            wmat[l, :, 384:768] = c2
            return carry

        lax.fori_loop(0, 3, line, 0)

    lane128 = iota((128, 128), 0)
    gather_mat = (iota((128, 128), 1) == b * 8 + lane128 // 16).astype(F32).astype(BF16)
    bin_mask = [(iota((8, 128), 1) // 8 == sub + 8 * h) for h in range(2)]

    def coarse_start(k):
        sums = jnp.zeros((8, 128), F32)
        for c in range(3):
            acc = None
            for x in range(16):
                term = (r[c, x, 0:8, :] + r[c, x, 8:16, :]) * float(SHARE[x % 8])
                acc = term if acc is None else acc + term
            line = jnp.sum(acc * syz, axis=0, keepdims=True)
            sums = sums + jnp.where(sub == c, jnp.broadcast_to(line, (8, 128)), 0.0)
        placed = exact_product(sums, gather_mat)
        row = placed[0:1]
        row = row + pltpu.roll(placed[1:2], 40, 1) + pltpu.roll(placed[2:3], 80, 1)
        rcs[k] = row

        def send(de, row_id, col):
            pltpu.make_async_remote_copy(
                src_ref=rcs.at[k],
                dst_ref=crecv.at[k, (1 - de) * n_bin + b],
                send_sem=csend.at[k],
                recv_sem=crsem.at[k],
                device_id=(row_id, col),
                device_id_type=MESH,
            ).start()

        each_partner(send)

    def coarse_finish(k):
        pltpu.make_async_copy(
            crecv.at[k, pl.ds(0, total)], crecv.at[k, pl.ds(0, total)], crsem.at[k]
        ).wait()
        crecv[k, n_bin + b] = rcs[k]
        rows = crecv[k].reshape(3 * n_bin, 128)
        spread = []
        for l in range(3):
            rc = jnp.zeros((8, 128), F32)
            for c in range(3):
                acc = None
                for h in range(2):
                    part = rows[l * 16 + 8 * h : l * 16 + 8 * h + 8]
                    if c:
                        part = pltpu.roll(part, 128 - 40 * c, 1)
                    part = jnp.where(bin_mask[h], part, 0.0)
                    acc = part if acc is None else acc + part
                line = jnp.sum(acc, axis=0, keepdims=True)
                rc = rc + jnp.where(sub == c, jnp.broadcast_to(line, (8, 128)), 0.0)
            out = mm(jnp.concatenate(split2(rc), 0), wmat[l])
            spread.append(out[0:8, 0:384] + out[8:16, 0:384] + out[0:8, 384:768])
        low, here, high = spread
        classes = (
            (0.5 * COARSE_GAIN) * (here + low),
            COARSE_GAIN * here,
            (0.5 * COARSE_GAIN) * (here + high),
        )
        for c in range(3):
            fill = []
            for value in classes:
                wide = lambda yc: jnp.broadcast_to(
                    value[c : c + 1, yc * 128 : (yc + 1) * 128], (8, 128)
                )
                middle = wide(1)
                fill.append(
                    (jnp.where(first_sub, wide(0), middle), jnp.where(last_sub, wide(2), middle))
                )
            for x in range(16):
                which = 0 if x == 0 else (2 if x == 15 else 1)
                for half in range(2):
                    rows8 = pl.ds(8 * half, 8)
                    step = dinv[x, rows8, :] * r[c, x, rows8, :] + fill[which][half]
                    if k:
                        step = step + vel[c, x, rows8, :]
                    vel[c, x, rows8, :] = step

    def operator(c, carry):
        v_all = vel[c].reshape(256, 128)
        grad = lane_product(v_all, ztab[0]) * coef[...].reshape(256, 128)
        r[c] = lane_product(grad, ztab[1]).reshape(16, 16, 128)
        for part in range(2):
            for half in range(2):
                rows = pl.ds(8 * half, 8)
                v = [vel[c, 8 * part + i, rows, :] for i in range(8)]
                cf = [coef[8 * part + i, rows, :] for i in range(8)]
                out = [r[c, 8 * part + i, rows, :] for i in range(8)]
                for i in range(8):
                    gx = float(DERIV[i, 0]) * v[0]
                    for k in range(1, 8):
                        if DERIV[i, k] != 0:
                            gx = gx + float(DERIV[i, k]) * v[k]
                    gx = gx * cf[i]
                    for k in range(8):
                        if DERIV[i, k] != 0:
                            out[k] = out[k] + float(DERIV[i, k]) * gx
                for i in range(8):
                    gy = contract_rows(v[i], 2) * cf[i]
                    total_q = out[i] + contract_rows(gy, 10)
                    lead = src[c, 8 * part + i, rows, :] - v[i]
                    r[c, 8 * part + i, rows, :] = (
                        lead * (wyz * float(WEIGHTS[i])) - total_q
                    )
        store_planes(
            c, lambda x: (r[c, x, 0:8, :], r[c, x, 8:16, :])
        )
        return carry

    share = TMAX // 8
    done = 0
    for k in range(ITERS):
        comps = 4 if k == 0 else 3
        if k:
            for copy in halos[k - 1]:
                copy.wait_send()
            lax.fori_loop(0, 3, operator, 0)
            halos[k] = halo_start(k, comps)
        tiles(done, share)
        done += share
        halo_finish(k, comps, halos[k])
        if k == 0:
            dinv[...] = RELAXATION / r[3]
        coarse_start(k)
        if k == 0:
            coarse_setup()
        tiles(done, share)
        done += share
        coarse_finish(k)

    means = jnp.zeros((8, 128), F32)
    for part in range(2):
        for half in range(2):
            rows = pl.ds(8 * half, 8)
            sums = jnp.zeros((8, 128), F32)
            for c in range(3):
                acc = None
                for i in range(8):
                    term = vel[c, 8 * part + i, rows, :] * float(WEIGHTS[i])
                    acc = term if acc is None else acc + term
                line = jnp.sum(acc * wyz, axis=0, keepdims=True)
                sums = sums + jnp.where(sub == c, jnp.broadcast_to(line, (8, 128)), 0.0)
            base = (part * 2 + half) * 16
            place = jnp.where(iota((128, 128), 1) == base + lane128 // 8, 0.125, 0.0)
            means = means + exact_product(sums, place.astype(BF16))
    parts = jnp.concatenate(split3(means[:, 0:64]), 0)

    def sample(i, carry):
        out = mm(parts, oh[i])
        samp[pl.ds(pl.multiple_of(i * 8, 8), 8), :] = out[0:8] + out[8:16] + out[16:24]
        return carry

    lax.fori_loop(0, NB, sample, 0)

    slot = iota((NB, TMAX), 1)
    hit = jnp.logical_and(
        jnp.broadcast_to(own_v[0:1, :], (NB, TMAX)) == iota((NB, TMAX), 0), slot < cnt_s[0]
    )
    hit = hit.astype(F32).astype(BF16)
    sums = []
    for c in range(4):
        value = raw[pl.ds(c, TMAX, stride=16), :]
        value = value + raw[pl.ds(4 + c, TMAX, stride=16), :]
        value = value + raw[pl.ds(8 + c, TMAX, stride=16), :]
        out = mm(hit, jnp.concatenate(split3(value), 1))
        sums.append(out[:, 0:128] + out[:, 128:256] + out[:, 256:384])
    size = drops[6]
    for c in range(3):
        position = drops[c] - 0.5
        force = STIFFNESS * size * (position * sums[0] - sums[1 + c])
        speed = drops[3 + c]
        sampled = samp[pl.ds(c, NB, stride=8), :]
        dvel[c] = speed + TIME_STEP * ((sampled - speed) / (size * size) + force)

    for copy in halos[ITERS - 1]:
        copy.wait_send()
    for copy in ghosts:
        copy.wait_send()
    pltpu.make_async_copy(
        xgat.at[pl.ds(0, total)], xgat.at[pl.ds(0, total)], xssem.at[0]
    ).wait()
    for k in range(ITERS):
        pltpu.make_async_copy(
            crecv.at[k, pl.ds(0, total)], crecv.at[k, pl.ds(0, total)], csend.at[k]
        ).wait()


def body(
    n_elem,
    n_bin,
    source,
    viscosity,
    coarse_inverse,
    droplets,
    droplet_elem,
    ghost_counts,
    tile_pairs,
    tile_count,
):
    tp = tile_pairs.reshape(2, TMAX)
    vmem = pl.BlockSpec(memory_space=pltpu.VMEM)
    smem = pl.BlockSpec(memory_space=pltpu.SMEM)
    dma = pltpu.SemaphoreType.DMA
    velocity, updated = pl.pallas_call(
        functools.partial(kernel, n_elem, n_bin),
        out_shape=(
            jax.ShapeDtypeStruct((3, 16, 16, 128), F32),
            jax.ShapeDtypeStruct((3, NB, 128), F32),
        ),
        in_specs=[smem] * 3 + [vmem] * 8,
        out_specs=(vmem, vmem),
        scratch_shapes=[
            pltpu.VMEM((16, 16, 128), F32),
            pltpu.VMEM((16, 16, 128), F32),
            pltpu.VMEM((4, 16, 16, 128), F32),
            pltpu.VMEM((4, 16, 16, 128), F32),
            pltpu.VMEM((ITERS, 2, 64, 128), F32),
            pltpu.VMEM((ITERS, 4, 4, 128), F32),
            pltpu.VMEM((ITERS, 2, 4, 16, 128), F32),
            pltpu.VMEM((ITERS, 2, 64, 128), F32),
            pltpu.VMEM((ITERS, 4, 4, 128), F32),
            pltpu.VMEM((ITERS, 1, 128), F32),
            pltpu.VMEM((ITERS, 3 * n_bin, 1, 128), F32),
            pltpu.VMEM((8, 128), F32),
            pltpu.VMEM((3 * n_bin, 8, 128), F32),
            pltpu.VMEM((3, 128, 768), BF16),
            pltpu.VMEM((2, 4, GMAX, 128), F32),
            pltpu.VMEM((2, 4, GMAX, 128), F32),
            pltpu.VMEM((NB * KF, 128), F32),
            pltpu.VMEM((NCAND * KF, 128), F32),
            pltpu.VMEM((NCAND * 16, 128), F32),
            pltpu.VMEM((NB, KF, 128), BF16),
            pltpu.VMEM((NCAND, 128, KF), BF16),
            pltpu.VMEM((NCAND, 16, 256), BF16),
            pltpu.VMEM((TMAX * 16, 128), F32),
            pltpu.VMEM((NB, 64, 128), BF16),
            pltpu.VMEM((NB * 8, 128), F32),
            dma((ITERS, 8)),
            dma((ITERS, 8)),
            dma((ITERS,)),
            dma((ITERS,)),
            dma((1,)),
            dma((1,)),
            dma((2,)),
            dma((2,)),
        ],
        compiler_params=pltpu.CompilerParams(
            collective_id=0, has_side_effects=True, vmem_limit_bytes=48 * 1024 * 1024
        ),
        name="sweeps",
    )(
        tp,
        tile_count.reshape(1),
        ghost_counts.reshape(2),
        source,
        viscosity,
        coarse_inverse,
        droplets.reshape(7, NB, 128),
        droplet_elem.reshape(NB, 128),
        tp,
        jnp.asarray(vector_tables()),
        jnp.asarray(lane_tables()),
    )
    return velocity, updated.reshape(3, 1, NB * 128)


def solution(mesh):
    in_specs = (
        P(None, "elem", "bin", None),
        P("elem", "bin", None),
        P("elem", "bin", None),
        P(None, "elem", "bin"),
        P("elem", "bin"),
        P(None, "elem", "bin"),
        P(None, "elem", "bin"),
        P("elem", "bin"),
    )
    out_specs = (P(None, "elem", "bin", None), P(None, "elem", "bin"))
    run = functools.partial(body, mesh.shape["elem"], mesh.shape["bin"])
    return jax.shard_map(run, mesh=mesh, in_specs=in_specs, out_specs=out_specs, check_vma=False)
```
